512 devices in a mesh: dom: 64 (over y, z_hi, x, core), feat: 8 (over z_lo).
Axes of the slice: x: 4, y: 4, z: 16 (z_hi: 2, z_lo: 8; z = z_hi * 8 + z_lo), core: 2. Of those that a mesh axis runs over, the one named last changes fastest.
Arguments:
- features: bfloat16 [32768, 1024], P('dom', 'feat'), may hold values from -16 to 16
- weights: bfloat16 [2048, 1024], P(None, 'feat'), may hold values from -4 to 4
- send_rows: int32 [64, 64, 128], P('dom'), may hold values from -1 to 511, as said below
- remote_src: int32 [64, 64], P('dom'), may hold values from 0 to 63, each once within a row
- local_adj: bfloat16 [32768, 512], P('dom')
- remote_adj: bfloat16 [32768, 16, 128], P('dom')
- degree: int32 [32768], P('dom'), may hold values from 48 to 143
- cotangent: bfloat16 [32768, 1024], P('dom', 'feat'), may hold values from -6 to 6
Outputs:
- output: bfloat16 [32768, 1024], P('dom', 'feat')
- grad_input: bfloat16 [32768, 1024], P('dom', 'feat')
- grad_weights: float32 [2048, 1024], P('dom', 'feat')
The draws below stay inside these ranges and needn't reach their ends.
Inputs may be any that keep to these rules, and one draw needn't show every extreme that they name: `send_rows`: each entry is a row of partition p or -1; in each block the used places come first and name distinct rows; a quarter or more of each block is used, and some block is full. `remote_src`: each row names every partition once.
All inputs are finite; a program needn't handle non-finite values.
Results may differ from the reference program's by a relative error of at most 0.01.
Values may be sent and summed in bfloat16 or wider, within the bound.
A program may use at most 64 MiB of HBM per device.

```python
import math
import jax
import jax.numpy as jnp
from jax import lax

H = 1024
BLK = 128
NBLK = 4
RT = 16
NP = 512
NODES = 32768
N_DOM = 64


def draw_weights(key, part):
    row_ids = jnp.arange(2 * H)[:, None]
    row_scale = jnp.where(row_ids >= H, 8.0, 1.0) / jnp.sqrt(jnp.float32(H))
    values = jnp.clip(jax.random.normal(jax.random.fold_in(key, 41), (2 * H, H), jnp.float32), -4.0, 4.0)
    return (values * row_scale).astype(jnp.bfloat16)


def draw_send_rows(key, part):
    key_rows = jax.random.fold_in(key, 11)
    key_count = jax.random.fold_in(key, 12)
    key_full = jax.random.fold_in(key, 13)
    slot_total = N_DOM * N_DOM
    slot_keys = jax.random.split(key_rows, slot_total)
    chosen = jax.vmap(lambda k: jax.random.permutation(k, NBLK * BLK)[:BLK])(slot_keys).astype(jnp.int32)
    counts = jax.random.randint(key_count, (slot_total,), BLK // 4, BLK + 1)
    full_slot = jax.random.randint(key_full, (), 0, slot_total)
    counts = jnp.where(jnp.arange(slot_total) == full_slot, BLK, counts)
    places = jnp.arange(BLK)
    filled = jnp.where(places[None, :] < counts[:, None], chosen, -1)
    return filled.reshape(N_DOM, N_DOM, BLK).astype(jnp.int32)


def draw_local_adj(key, part):
    picks = jax.random.randint(jax.random.fold_in(key, 21), (NODES, NBLK * BLK), 0, 16)
    return (picks == 0).astype(jnp.float32).astype(jnp.bfloat16)


def draw_remote_adj(key, part):
    picks = jax.random.randint(jax.random.fold_in(key, 31), (NODES, RT, BLK), 0, 32)
    return (picks == 0).astype(jnp.float32).astype(jnp.bfloat16)


def with_ends(array, rng, smallest, high):
    longest = array.shape.index(max(array.shape))
    spots = []
    for shift in (0, 1):
        where = [jax.random.randint(jax.random.fold_in(rng, axis), (), 0, length) for axis, length in enumerate(array.shape)]
        where[longest] = (where[longest] + shift) % array.shape[longest]
        spots.append(tuple(where))
    return array.at[spots[0]].set(smallest).at[spots[1]].set(high)


def raised(entries, own_key, source, target, blocks, factor):
    owner, partner = [(jnp.arange(entries.shape[axis_at]) // (entries.shape[axis_at] // blocks)).reshape([-1 if axis == axis_at else 1 for axis in range(entries.ndim)]) for axis_at in (source, target)]
    chosen = jax.random.permutation(own_key, blocks)[partner]
    strong = (owner == chosen) | (owner == (partner + blocks // 2) % blocks)
    return jnp.where(strong, factor * entries, entries)


def block_scale(key, dims, cuts, low, largest):
    level, own = 1.0, jax.random.fold_in(key, 6)
    for position, blocks in cuts:
        draws = jnp.exp(jax.random.uniform(jax.random.fold_in(own, position), (blocks,), jnp.float32, low / len(cuts), largest / len(cuts)))
        level = level * jnp.repeat(draws, dims[position] // blocks).reshape([-1 if axis == position else 1 for axis in range(len(dims))])
    return level


def scatter_about(rng, dims, deviation, most, cuts=(), kind=jnp.bfloat16):
    result = deviation * jax.random.normal(rng, dims, jnp.float32)
    if cuts:
        result = result * block_scale(rng, dims, cuts, -0.22, 0.18)
    return jnp.clip(result, -most, most).astype(kind)


def heavy_noise(stream_key, extent, width, limit, shards, heavy, held_as=jnp.bfloat16):
    drawn = width * jax.random.normal(stream_key, extent, jnp.float32)
    if shards:
        drawn = drawn * block_scale(stream_key, extent, shards, -0.22, 0.18)
    return jnp.clip(raised(drawn, jax.random.fold_in(stream_key, 3), *heavy), -limit, limit).astype(held_as)


def setup_inputs(seed: int = 0) -> dict:
    keys = jax.random.split(jax.random.key(seed), 9)
    return {
        "features": heavy_noise(keys[0], (NODES, H), 1.0, 16.0, ((0, 64), (1, 8)), (0, 1, 64, 4.0)),
        "weights": draw_weights(jax.random.fold_in(keys[8], 71), 0),
        "send_rows": draw_send_rows(jax.random.fold_in(keys[8], 71), 0),
        "remote_src": jax.vmap(lambda own: jax.random.permutation(own, N_DOM))(jax.random.split(keys[3], N_DOM)).reshape((N_DOM, N_DOM)).astype(jnp.int32),
        "local_adj": draw_local_adj(jax.random.fold_in(keys[8], 71), 0),
        "remote_adj": draw_remote_adj(jax.random.fold_in(keys[8], 71), 0),
        "degree": with_ends(jax.random.randint(keys[6], (NODES,), 48, 144), jax.random.fold_in(keys[6], 1), 48, 143).astype(jnp.int32),
        "cotangent": scatter_about(keys[7], (NODES, H), 1.0, 6.0, ((0, 64), (1, 8))),
    }


def reference(features, weights, send_rows, remote_src, local_adj, remote_adj, degree, cotangent):
    node_parts = features.reshape(N_DOM, NP, H)
    degree_col = degree.astype(jnp.float32)[:, None]
    degree_parts = degree_col.reshape(N_DOM, NP, 1)
    local_parts = local_adj.reshape(N_DOM, NP, NP)
    tile_parts = remote_adj.reshape(N_DOM, NBLK, BLK, RT * BLK)
    part_ids = jnp.arange(N_DOM, dtype=jnp.int32)

    def halo_of(target):
        wanted = send_rows[:, target, :]
        live_mask = wanted >= 0
        safe_rows = jnp.where(live_mask, wanted, 0)
        picked = node_parts[part_ids[:, None], safe_rows]
        return jnp.where(live_mask[:, :, None], picked, jnp.zeros_like(picked))

    def forward_part(target):
        halo_rows = halo_of(target)
        ordered = halo_rows[remote_src[target]].reshape(NBLK, RT * BLK, H)
        remote_sums = jnp.einsum('bik,bkf->bif', tile_parts[target].astype(jnp.float32), ordered.astype(jnp.float32)).reshape(NP, H)
        local_sums = jnp.dot(local_parts[target], node_parts[target], preferred_element_type=jnp.float32)
        return ((local_sums + remote_sums) / degree_parts[target]).astype(jnp.bfloat16)
    aggregate = lax.map(forward_part, part_ids).reshape(NODES, H)
    combined = jnp.concatenate([features, aggregate], axis=1)
    preact = jnp.dot(combined, weights, preferred_element_type=jnp.float32)
    output = jax.nn.silu(preact).astype(jnp.bfloat16)
    sigmoid_z = jax.nn.sigmoid(preact)
    grad_pre = (cotangent.astype(jnp.float32) * sigmoid_z * (1.0 + preact * (1.0 - sigmoid_z))).astype(jnp.bfloat16)
    scaled_grad = (grad_pre.astype(jnp.float32) / degree_col).astype(jnp.bfloat16)
    scaled_parts = scaled_grad.reshape(N_DOM, NP, H)

    def backward_part(carried, target):
        own = scaled_parts[target]
        ordered = jnp.einsum('bik,bif->bkf', tile_parts[target].astype(jnp.float32), own.reshape(NBLK, BLK, H).astype(jnp.float32))
        returned = ordered.reshape(N_DOM, BLK, H).astype(jnp.bfloat16).astype(jnp.float32)
        sources = remote_src[target]
        wanted = send_rows[sources, target, :]
        safe_rows = jnp.where(wanted >= 0, wanted, NP)
        carried = carried.at[sources[:, None], safe_rows].add(returned, mode='drop')
        local_term = lax.dot_general(local_parts[target], own, (((0,), (0,)), ((), ())), preferred_element_type=jnp.float32)
        carried = carried.at[target].add(local_term)
        return (carried, None)
    neigh_grad, _ = lax.scan(backward_part, jnp.zeros((N_DOM, NP, H), jnp.float32), part_ids)
    neigh_grad = neigh_grad.reshape(NODES, H).astype(jnp.bfloat16)
    self_term = jnp.dot(grad_pre, weights[:H].T, preferred_element_type=jnp.float32)
    neigh_term = jnp.dot(neigh_grad, weights[H:].T, preferred_element_type=jnp.float32)
    grad_input = (self_term + neigh_term).astype(jnp.bfloat16)
    grad_weights = jnp.dot(combined.T, grad_pre, preferred_element_type=jnp.float32) / math.sqrt(NODES)
    return (output, grad_input, grad_weights)
```

```python
import math

import jax
import jax.numpy as jnp
from jax import lax
from jax.experimental import pallas as pl
from jax.experimental.pallas import tpu as pltpu
from jax.sharding import PartitionSpec as P

BF = jnp.bfloat16
F32 = jnp.float32
VMEM_BYTES = 48 * 1024 * 1024
NT = (((1,), (1,)), ((), ()))


def vmem():
    return pl.BlockSpec(memory_space=pltpu.VMEM)


def smem():
    return pl.BlockSpec(memory_space=pltpu.SMEM)


def params():
    return pltpu.CompilerParams(vmem_limit_bytes=VMEM_BYTES)


def one_hot(rows, count):
    spots = lax.broadcasted_iota(jnp.int32, (count, rows.shape[1]), 0)
    return jnp.where(spots == rows, 1.0, 0.0).astype(BF)


def pack_kernel(ft_ref, rows_ref, out_ref):
    count = ft_ref.shape[2]
    for z in range(2):
        ft = ft_ref[z]

        def body(j, carry):
            picked = jnp.dot(ft, one_hot(rows_ref[j, pl.ds(z, 1), :], count), preferred_element_type=F32)
            out_ref[j, z] = picked.astype(BF)
            return carry

        lax.fori_loop(0, out_ref.shape[0], body, 0, unroll=4)


def agg_kernel(src_ref, local_ref, feat_ref, tiles_ref, halo_ref, deg_ref, agg_ref, ordered):
    blk = halo_ref.shape[1]
    blocks = local_ref.shape[0] // blk
    span = tiles_ref.shape[1] // blk

    def body(b, carry):
        for t in range(span):
            ordered[:, t * blk:(t + 1) * blk] = halo_ref[src_ref[b * span + t]]
        rows = pl.ds(pl.multiple_of(b * blk, blk), blk)
        sums = lax.dot_general(tiles_ref[rows, :], ordered[...], NT, preferred_element_type=F32)
        sums += jnp.dot(local_ref[rows, :], feat_ref[...], preferred_element_type=F32)
        agg_ref[rows, :] = (sums / deg_ref[rows, :]).astype(BF)
        return carry

    lax.fori_loop(0, blocks, body, 0)


def back_kernel(src_ref, scaled_t_ref, tiles_ref, back_ref):
    blk = back_ref.shape[1]
    blocks = scaled_t_ref.shape[1] // blk
    span = tiles_ref.shape[1] // blk
    for b in range(blocks):
        left = scaled_t_ref[:, b * blk:(b + 1) * blk]
        terms = jnp.dot(
            left, tiles_ref[b * blk:(b + 1) * blk, :], preferred_element_type=F32
        ).astype(BF)
        for t in range(span):
            back_ref[src_ref[b * span + t]] = terms[:, t * blk:(t + 1) * blk]


def unpack_kernel(rows_ref, arrived_ref, scaled_t_ref, local_ref, half_ref, own_ref, other_ref, total):
    count = local_ref.shape[1]
    half = half_ref[0]
    total[...] = jnp.zeros_like(total)
    for z in range(2):

        def body(j, carry):
            left = jnp.concatenate([arrived_ref[2 * j, z], arrived_ref[2 * j + 1, z]], axis=1)
            right = jnp.concatenate(
                [
                    one_hot(rows_ref[2 * j, pl.ds(z, 1), :], count),
                    one_hot(rows_ref[2 * j + 1, pl.ds(z, 1), :], count),
                ],
                axis=1,
            )
            total[z] += lax.dot_general(left, right, NT, preferred_element_type=F32)
            return carry

        lax.fori_loop(0, arrived_ref.shape[0] // 2, body, 0, unroll=2)
    local = jnp.dot(scaled_t_ref[...], local_ref[...], preferred_element_type=F32)
    own_ref[...] = local + total[half]
    other_ref[...] = total[1 - half].astype(BF)


def per_device(features, weights, send_rows, remote_src, local_adj, remote_adj, degree, cotangent):
    np_rows, width = features.shape
    feats = lax.axis_size("feat")
    doms = lax.axis_size("dom")
    blk = remote_adj.shape[2]
    span = remote_adj.shape[1] * blk
    half_count = doms // 2
    pair = 8
    half = (lax.axis_index("dom") // pair) % 2
    swaps = [(d, d ^ pair) for d in range(doms)]
    groups = [[d for d in range(doms) if (d // pair) % 2 == h] for h in range(2)]

    feat_t = features.T
    other_t = lax.ppermute(feat_t, "dom", swaps)
    rows_own = send_rows[0]
    rows_other = lax.ppermute(rows_own, "dom", swaps)

    def by_half(own, other):
        return jnp.where(half == 0, jnp.stack([own, other]), jnp.stack([other, own]))

    rows2 = by_half(rows_own, rows_other).reshape(2, doms // 16, 2, pair, blk)
    rows2 = jnp.where(half == 0, rows2[:, :, 0], rows2[:, :, 1]).reshape(2, half_count, blk)
    rows2 = rows2.transpose(1, 0, 2)
    packed = pl.pallas_call(
        pack_kernel,
        out_shape=jax.ShapeDtypeStruct((half_count, 2, width, blk), BF),
        in_specs=[vmem(), vmem()],
        out_specs=vmem(),
        compiler_params=params(),
    )(by_half(feat_t, other_t), rows2)
    halo = lax.all_to_all(
        packed, "dom", split_axis=0, concat_axis=0, tiled=True, axis_index_groups=groups
    ).reshape(doms, width, blk)

    src = remote_src[0]
    slots = ((src // 16) * pair + src % pair) * 2 + (src // pair) % 2
    tiles = remote_adj.reshape(np_rows, span)
    deg = jnp.broadcast_to(degree.astype(F32)[:, None], (np_rows, width))
    gathered_feat = lax.all_gather(features, "feat", axis=0)
    aggregate = pl.pallas_call(
        agg_kernel,
        out_shape=jax.ShapeDtypeStruct((np_rows, width), BF),
        in_specs=[smem()] + [vmem()] * 5,
        out_specs=vmem(),
        scratch_shapes=[pltpu.VMEM((width, span), BF)],
        compiler_params=params(),
    )(slots, local_adj, features, tiles, halo, deg)
    gathered_agg = lax.all_gather(aggregate, "feat", axis=0)

    full = width * feats
    w_pair = weights.reshape(2, feats, width, width)
    preact = jnp.einsum(
        "krf,kfc->rc", gathered_feat, w_pair[0], preferred_element_type=F32
    ) + jnp.einsum("krf,kfc->rc", gathered_agg, w_pair[1], preferred_element_type=F32)
    output = jax.nn.silu(preact).astype(BF)
    sig = jax.nn.sigmoid(preact)
    grad_pre = (cotangent.astype(F32) * sig * (1.0 + preact * (1.0 - sig))).astype(BF)
    scaled = (grad_pre.astype(F32) / deg).astype(BF)
    scaled_t = scaled.T

    back = pl.pallas_call(
        back_kernel,
        out_shape=jax.ShapeDtypeStruct((doms, width, blk), BF),
        in_specs=[smem(), vmem(), vmem()],
        out_specs=vmem(),
        compiler_params=params(),
    )(slots, scaled_t, tiles).reshape(half_count, 2, width, blk)
    arrived = lax.all_to_all(
        back, "dom", split_axis=0, concat_axis=0, tiled=True, axis_index_groups=groups
    )
    own_term, other_term = pl.pallas_call(
        unpack_kernel,
        out_shape=(
            jax.ShapeDtypeStruct((width, np_rows), F32),
            jax.ShapeDtypeStruct((width, np_rows), BF),
        ),
        in_specs=[vmem()] * 4 + [smem()],
        out_specs=(vmem(), vmem()),
        scratch_shapes=[pltpu.VMEM((2, width, np_rows), F32)],
        compiler_params=params(),
    )(rows2, arrived, scaled_t, local_adj, half.reshape(1).astype(jnp.int32))
    from_other = lax.ppermute(other_term, "dom", swaps)
    neigh_t = (own_term + from_other.astype(F32)).astype(BF)

    terms = jnp.einsum(
        "rf,kcf->krc", grad_pre, w_pair[0], preferred_element_type=F32
    ) + jnp.einsum("fr,kcf->krc", neigh_t, w_pair[1], preferred_element_type=F32)
    landed = lax.all_to_all(terms.astype(BF), "feat", split_axis=0, concat_axis=0, tiled=True)
    grad_input = jnp.sum(landed.astype(F32), axis=0).astype(BF)

    def weight_terms(left):
        return jnp.einsum("krf,rc->kfc", left, grad_pre, preferred_element_type=F32)

    share = jnp.stack([weight_terms(gathered_feat), weight_terms(gathered_agg)])
    share = share.astype(BF).reshape(doms, 2 * full // doms, width)
    shares = lax.all_to_all(share, "dom", split_axis=0, concat_axis=0, tiled=True)
    weight_scale = 1.0 / math.sqrt(doms * np_rows)
    grad_weights = jnp.sum(shares.astype(F32), axis=0) * weight_scale
    return (output, grad_input, grad_weights)


def solution(mesh):
    in_specs = (
        P("dom", "feat"),
        P(None, "feat"),
        P("dom", None, None),
        P("dom", None),
        P("dom", None),
        P("dom", None, None),
        P("dom"),
        P("dom", "feat"),
    )
    out_specs = (P("dom", "feat"), P("dom", "feat"), P("dom", "feat"))
    return jax.shard_map(
        per_device, mesh=mesh, in_specs=in_specs, out_specs=out_specs, check_vma=False
    )
```

```python
import math

import jax
import jax.numpy as jnp
from jax import lax
from jax.experimental import pallas as pl
from jax.experimental.pallas import tpu as pltpu
from jax.sharding import PartitionSpec as P

BF = jnp.bfloat16
F32 = jnp.float32
VMEM_BYTES = 48 * 1024 * 1024
PAIR = 8
NT = (((1,), (1,)), ((), ()))


def vmem():
    return pl.BlockSpec(memory_space=pltpu.VMEM)


def smem():
    return pl.BlockSpec(memory_space=pltpu.SMEM)


def params():
    return pltpu.CompilerParams(vmem_limit_bytes=VMEM_BYTES)


def linked(number):
    return pltpu.CompilerParams(
        vmem_limit_bytes=VMEM_BYTES, collective_id=number, has_side_effects=True
    )


def one_hot(rows, count):
    spots = lax.broadcasted_iota(jnp.int32, (count, rows.shape[1]), 0)
    return jnp.where(spots == rows, 1.0, 0.0).astype(BF)


def pack_kernel(ft_ref, rows_ref, out_ref):
    count = ft_ref.shape[2]
    for z in range(2):
        ft = ft_ref[z]

        def body(j, carry):
            picked = jnp.dot(ft, one_hot(rows_ref[j, pl.ds(z, 1), :], count), preferred_element_type=F32)
            out_ref[j, z] = picked.astype(BF)
            return carry

        lax.fori_loop(0, out_ref.shape[0], body, 0, unroll=4)


def enter(partner=None):
    me = lax.axis_index("feat")
    feats = lax.axis_size("feat")
    barrier = pltpu.get_barrier_semaphore()
    places = [{"feat": lax.rem(me + 1, feats)}, {"feat": lax.rem(me + feats - 1, feats)}]
    if partner is not None:
        places.append({"dom": partner})
    for place in places:
        pl.semaphore_signal(barrier, inc=1, device_id=place, device_id_type=pl.DeviceIdType.MESH)
    pl.semaphore_wait(barrier, len(places))


class LineGather:
    def __init__(self, own, blocks, send, recv):
        self.own, self.blocks, self.send, self.recv = own, blocks, send, recv
        self.me = lax.axis_index("feat")
        self.last = lax.axis_size("feat") - 1

    def copy(self, way, step, coming=0):
        up = way == 0
        back = step + coming
        source = jnp.clip(self.me - back if up else self.me + back, 0, self.last)
        target = jnp.clip(self.me + 1 if up else self.me - 1, 0, self.last)
        return pltpu.make_async_remote_copy(
            src_ref=self.own if back == 0 else self.blocks.at[source],
            dst_ref=self.blocks.at[source],
            send_sem=self.send.at[way, step],
            recv_sem=self.recv.at[way, step],
            device_id={"feat": target},
            device_id_type=pl.DeviceIdType.MESH,
        )

    def sends(self, way, step):
        if way == 0:
            return jnp.logical_and(self.me >= step, self.me < self.last)
        return jnp.logical_and(self.me <= self.last - step, self.me > 0)

    def gets(self, way, step):
        return self.me > step if way == 0 else self.me < self.last - step

    def start(self, step):
        for way in range(2):

            @pl.when(self.sends(way, step))
            def _():
                self.copy(way, step).start()

    def arrive(self, step):
        for way in range(2):

            @pl.when(self.gets(way, step))
            def _():
                self.copy(way, step, 1).wait_recv()

    def finish(self):
        for step in range(self.last):
            for way in range(2):

                @pl.when(self.sends(way, step))
                def _():
                    self.copy(way, step).wait_send()


def run_lines(lines):
    last = lines[0].last
    for step in range(last):
        for line in lines:
            line.arrive(step)
            if step + 1 < last:
                line.start(step + 1)
    for line in lines:
        line.finish()


def line_scratch(feats, rows, width):
    return [
        pltpu.VMEM((feats, rows, width), BF),
        pltpu.SemaphoreType.DMA((2, feats - 1)),
        pltpu.SemaphoreType.DMA((2, feats - 1)),
    ]


def agg_kernel(
    src_ref, local_ref, feat_ref, tiles_ref, halo_ref, deg_ref, all_feat_ref, all_agg_ref,
    ordered, agg_ref, held_feat, send_feat, recv_feat, held_agg, send_agg, recv_agg,
):
    me = lax.axis_index("feat")
    enter()
    feat_line = LineGather(feat_ref, held_feat, send_feat, recv_feat)
    agg_line = LineGather(agg_ref, held_agg, send_agg, recv_agg)
    feat_line.start(0)
    blk = halo_ref.shape[1]
    blocks = local_ref.shape[0] // blk
    span = tiles_ref.shape[1] // blk

    def body(b, carry):
        for t in range(span):
            ordered[:, t * blk:(t + 1) * blk] = halo_ref[src_ref[b * span + t]]
        rows = pl.ds(pl.multiple_of(b * blk, blk), blk)
        sums = lax.dot_general(tiles_ref[rows, :], ordered[...], NT, preferred_element_type=F32)
        sums += jnp.dot(local_ref[rows, :], feat_ref[...], preferred_element_type=F32)
        agg_ref[rows, :] = (sums / deg_ref[rows, :]).astype(BF)
        return carry

    lax.fori_loop(0, blocks, body, 0)
    agg_line.start(0)
    held_feat[me] = feat_ref[...]
    held_agg[me] = agg_ref[...]
    run_lines([feat_line, agg_line])
    for k in range(held_feat.shape[0]):
        all_feat_ref[k] = held_feat[k]
        all_agg_ref[k] = held_agg[k]


def back_kernel(src_ref, scaled_t_ref, tiles_ref, back_ref):
    blk = back_ref.shape[1]
    blocks = scaled_t_ref.shape[1] // blk
    span = tiles_ref.shape[1] // blk
    for b in range(blocks):
        left = scaled_t_ref[:, b * blk:(b + 1) * blk]
        terms = jnp.dot(
            left, tiles_ref[b * blk:(b + 1) * blk, :], preferred_element_type=F32
        ).astype(BF)
        for t in range(span):
            back_ref[src_ref[b * span + t]] = terms[:, t * blk:(t + 1) * blk]


def unpack_kernel(
    rows_ref, arrived_ref, scaled_t_ref, local_ref, grad_ref, all_grad_ref, all_neigh_ref,
    total, other_ref, landed_ref, neigh_ref, swap_send, swap_recv,
    held_grad, send_grad, recv_grad, held_neigh, send_neigh, recv_neigh,
):
    me = lax.axis_index("feat")
    dom = lax.axis_index("dom")
    count = local_ref.shape[1]
    half = lax.rem(dom // PAIR, 2)
    partner = dom + PAIR * (1 - 2 * half)
    enter(partner)
    grad_line = LineGather(grad_ref, held_grad, send_grad, recv_grad)
    neigh_line = LineGather(neigh_ref, held_neigh, send_neigh, recv_neigh)
    grad_line.start(0)
    total[...] = jnp.zeros_like(total)
    for z in range(2):

        def body(j, carry):
            left = jnp.concatenate([arrived_ref[2 * j, z], arrived_ref[2 * j + 1, z]], axis=1)
            right = jnp.concatenate(
                [
                    one_hot(rows_ref[2 * j, pl.ds(z, 1), :], count),
                    one_hot(rows_ref[2 * j + 1, pl.ds(z, 1), :], count),
                ],
                axis=1,
            )
            total[z] += lax.dot_general(left, right, NT, preferred_element_type=F32)
            return carry

        lax.fori_loop(0, arrived_ref.shape[0] // 2, body, 0, unroll=2)
    other_ref[...] = total[1 - half].astype(BF)
    swap = pltpu.make_async_remote_copy(
        src_ref=other_ref,
        dst_ref=landed_ref,
        send_sem=swap_send,
        recv_sem=swap_recv,
        device_id={"dom": partner},
        device_id_type=pl.DeviceIdType.MESH,
    )
    swap.start()
    held_grad[me] = grad_ref[...]
    local = jnp.dot(scaled_t_ref[...], local_ref[...], preferred_element_type=F32)
    total[half] += local
    run_first = 2
    for step in range(run_first):
        grad_line.arrive(step)
        grad_line.start(step + 1)
    swap.wait()
    neigh = (total[half] + landed_ref[...].astype(F32)).astype(BF)
    neigh_ref[...] = neigh
    neigh_line.start(0)
    held_neigh[me] = neigh
    last = grad_line.last
    for step in range(last):
        if step >= run_first:
            grad_line.arrive(step)
            if step + 1 < last:
                grad_line.start(step + 1)
        neigh_line.arrive(step)
        if step + 1 < last:
            neigh_line.start(step + 1)
    grad_line.finish()
    neigh_line.finish()
    for k in range(held_grad.shape[0]):
        all_grad_ref[k] = held_grad[k]
        all_neigh_ref[k] = held_neigh[k]


def per_device(features, weights, send_rows, remote_src, local_adj, remote_adj, degree, cotangent):
    np_rows, width = features.shape
    feats = lax.axis_size("feat")
    doms = lax.axis_size("dom")
    blk = remote_adj.shape[2]
    span = remote_adj.shape[1] * blk
    half_count = doms // 2
    pair = PAIR
    half = (lax.axis_index("dom") // pair) % 2
    swaps = [(d, d ^ pair) for d in range(doms)]
    groups = [[d for d in range(doms) if (d // pair) % 2 == h] for h in range(2)]

    feat_t = features.T
    other_t = lax.ppermute(feat_t, "dom", swaps)
    rows_own = send_rows[0]
    rows_other = lax.ppermute(rows_own, "dom", swaps)

    def by_half(own, other):
        return jnp.where(half == 0, jnp.stack([own, other]), jnp.stack([other, own]))

    rows2 = by_half(rows_own, rows_other).reshape(2, doms // 16, 2, pair, blk)
    rows2 = jnp.where(half == 0, rows2[:, :, 0], rows2[:, :, 1]).reshape(2, half_count, blk)
    rows2 = rows2.transpose(1, 0, 2)
    packed = pl.pallas_call(
        pack_kernel,
        out_shape=jax.ShapeDtypeStruct((half_count, 2, width, blk), BF),
        in_specs=[vmem(), vmem()],
        out_specs=vmem(),
        compiler_params=params(),
    )(by_half(feat_t, other_t), rows2)
    halo = lax.all_to_all(
        packed, "dom", split_axis=0, concat_axis=0, tiled=True, axis_index_groups=groups
    ).reshape(doms, width, blk)

    w_pair = weights.reshape(2, feats, width, width)
    w_rows = lax.all_to_all(
        w_pair.transpose(1, 0, 2, 3), "feat", split_axis=0, concat_axis=0, tiled=True
    )

    src = remote_src[0]
    slots = ((src // 16) * pair + src % pair) * 2 + (src // pair) % 2
    tiles = remote_adj.reshape(np_rows, span)
    deg = jnp.broadcast_to(degree.astype(F32)[:, None], (np_rows, width))
    gathered_feat, gathered_agg = pl.pallas_call(
        agg_kernel,
        out_shape=(jax.ShapeDtypeStruct((feats, np_rows, width), BF),) * 2,
        in_specs=[smem()] + [vmem()] * 5,
        out_specs=(vmem(), vmem()),
        scratch_shapes=[pltpu.VMEM((width, span), BF), pltpu.VMEM((np_rows, width), BF)]
        + line_scratch(feats, np_rows, width) * 2,
        compiler_params=linked(1),
    )(slots, local_adj, features, tiles, halo, deg)

    full = width * feats
    preact = jnp.einsum(
        "krf,kfc->rc", gathered_feat, w_pair[0], preferred_element_type=F32
    ) + jnp.einsum("krf,kfc->rc", gathered_agg, w_pair[1], preferred_element_type=F32)
    output = jax.nn.silu(preact).astype(BF)
    sig = jax.nn.sigmoid(preact)
    grad_pre = (cotangent.astype(F32) * sig * (1.0 + preact * (1.0 - sig))).astype(BF)
    scaled = (grad_pre.astype(F32) / deg).astype(BF)
    scaled_t = scaled.T

    back = pl.pallas_call(
        back_kernel,
        out_shape=jax.ShapeDtypeStruct((doms, width, blk), BF),
        in_specs=[smem(), vmem(), vmem()],
        out_specs=vmem(),
        compiler_params=params(),
    )(slots, scaled_t, tiles).reshape(half_count, 2, width, blk)
    arrived = lax.all_to_all(
        back, "dom", split_axis=0, concat_axis=0, tiled=True, axis_index_groups=groups
    )
    gathered_grad, gathered_neigh = pl.pallas_call(
        unpack_kernel,
        out_shape=(
            jax.ShapeDtypeStruct((feats, np_rows, width), BF),
            jax.ShapeDtypeStruct((feats, width, np_rows), BF),
        ),
        in_specs=[vmem()] * 5,
        out_specs=(vmem(), vmem()),
        scratch_shapes=[
            pltpu.VMEM((2, width, np_rows), F32),
            pltpu.VMEM((width, np_rows), BF),
            pltpu.VMEM((width, np_rows), BF),
            pltpu.VMEM((width, np_rows), BF),
            pltpu.SemaphoreType.DMA,
            pltpu.SemaphoreType.DMA,
        ]
        + line_scratch(feats, np_rows, width)
        + line_scratch(feats, width, np_rows),
        compiler_params=linked(2),
    )(rows2, arrived, scaled_t, local_adj, grad_pre)
    grad_input = (
        jnp.einsum("krc,kfc->rf", gathered_grad, w_rows[:, 0], preferred_element_type=F32)
        + jnp.einsum("kcr,kfc->rf", gathered_neigh, w_rows[:, 1], preferred_element_type=F32)
    ).astype(BF)

    def weight_terms(left):
        return jnp.einsum("krf,rc->kfc", left, grad_pre, preferred_element_type=F32)

    share = jnp.stack([weight_terms(gathered_feat), weight_terms(gathered_agg)])
    share = share.astype(BF).reshape(doms, 2 * full // doms, width)
    shares = lax.all_to_all(share, "dom", split_axis=0, concat_axis=0, tiled=True)
    weight_scale = 1.0 / math.sqrt(doms * np_rows)
    grad_weights = jnp.sum(shares.astype(F32), axis=0) * weight_scale
    return (output, grad_input, grad_weights)


def solution(mesh):
    in_specs = (
        P("dom", "feat"),
        P(None, "feat"),
        P("dom", None, None),
        P("dom", None),
        P("dom", None),
        P("dom", None, None),
        P("dom"),
        P("dom", "feat"),
    )
    out_specs = (P("dom", "feat"), P("dom", "feat"), P("dom", "feat"))
    return jax.shard_map(
        per_device, mesh=mesh, in_specs=in_specs, out_specs=out_specs, check_vma=False
    )
```

```python
import math

import jax
import jax.numpy as jnp
from jax import lax
from jax.experimental import pallas as pl
from jax.experimental.pallas import tpu as pltpu
from jax.sharding import PartitionSpec as P

BF = jnp.bfloat16
F32 = jnp.float32
VMEM_BYTES = 48 * 1024 * 1024
PAIR = 8
NT = (((1,), (1,)), ((), ()))


def vmem():
    return pl.BlockSpec(memory_space=pltpu.VMEM)


def smem():
    return pl.BlockSpec(memory_space=pltpu.SMEM)


def params():
    return pltpu.CompilerParams(vmem_limit_bytes=VMEM_BYTES)


def linked(number):
    return pltpu.CompilerParams(
        vmem_limit_bytes=VMEM_BYTES, collective_id=number, has_side_effects=True
    )


def one_hot(rows, count):
    spots = lax.broadcasted_iota(jnp.int32, (count, rows.shape[1]), 0)
    return jnp.where(spots == rows, 1.0, 0.0).astype(BF)


def signal(place):
    pl.semaphore_signal(
        pltpu.get_barrier_semaphore(), inc=1, device_id=place, device_id_type=pl.DeviceIdType.MESH
    )


class Seat:
    def __init__(self):
        self.dom = lax.axis_index("dom")
        self.mates = lax.axis_size("dom") // 2
        self.half = lax.rem(self.dom // PAIR, 2)
        self.partner = self.dom + PAIR * (1 - 2 * self.half)
        self.place = (self.dom // (2 * PAIR)) * PAIR + lax.rem(self.dom, PAIR)

    def mate(self, step):
        return lax.rem(self.place + step, self.mates)

    def dom_of(self, place):
        return (place // PAIR) * (2 * PAIR) + self.half * PAIR + lax.rem(place, PAIR)

    def enter(self):
        me = lax.axis_index("feat")
        feats = lax.axis_size("feat")
        signal({"feat": lax.rem(me + 1, feats)})
        signal({"feat": lax.rem(me + feats - 1, feats)})
        signal({"dom": self.partner})

        def body(step, carry):
            signal({"dom": self.dom_of(self.mate(step))})
            return carry

        lax.fori_loop(1, self.mates, body, 0)
        pl.semaphore_wait(pltpu.get_barrier_semaphore(), self.mates + 2)

    def swap(self, src, dst, send, recv):
        return pltpu.make_async_remote_copy(
            src_ref=src, dst_ref=dst, send_sem=send, recv_sem=recv,
            device_id={"dom": self.partner}, device_id_type=pl.DeviceIdType.MESH,
        )

    def mail(self, src, dst, send, recv, place):
        return pltpu.make_async_remote_copy(
            src_ref=src, dst_ref=dst, send_sem=send, recv_sem=recv,
            device_id={"dom": self.dom_of(place)}, device_id_type=pl.DeviceIdType.MESH,
        )

    def for_mates(self, act):
        def body(step, carry):
            act(step, self.mate(step))
            return carry

        lax.fori_loop(1, self.mates, body, 0)


class LineGather:
    def __init__(self, own, blocks, send, recv):
        self.own, self.blocks, self.send, self.recv = own, blocks, send, recv
        self.me = lax.axis_index("feat")
        self.last = lax.axis_size("feat") - 1

    def copy(self, way, step, coming=0):
        up = way == 0
        back = step + coming
        source = jnp.clip(self.me - back if up else self.me + back, 0, self.last)
        target = jnp.clip(self.me + 1 if up else self.me - 1, 0, self.last)
        return pltpu.make_async_remote_copy(
            src_ref=self.own if back == 0 else self.blocks.at[source],
            dst_ref=self.blocks.at[source],
            send_sem=self.send.at[way, step],
            recv_sem=self.recv.at[way, step],
            device_id={"feat": target},
            device_id_type=pl.DeviceIdType.MESH,
        )

    def sends(self, way, step):
        if way == 0:
            return jnp.logical_and(self.me >= step, self.me < self.last)
        return jnp.logical_and(self.me <= self.last - step, self.me > 0)

    def gets(self, way, step):
        return self.me > step if way == 0 else self.me < self.last - step

    def start(self, step):
        for way in range(2):

            @pl.when(self.sends(way, step))
            def _():
                self.copy(way, step).start()

    def arrive(self, step):
        for way in range(2):

            @pl.when(self.gets(way, step))
            def _():
                self.copy(way, step, 1).wait_recv()

    def finish(self):
        for step in range(self.last):
            for way in range(2):

                @pl.when(self.sends(way, step))
                def _():
                    self.copy(way, step).wait_send()


def run_lines(lines):
    last = lines[0].last
    for step in range(last):
        for line in lines:
            line.arrive(step)
            if step + 1 < last:
                line.start(step + 1)
    for line in lines:
        line.finish()


def line_scratch(feats, rows, width):
    return [
        pltpu.VMEM((feats, rows, width), BF),
        pltpu.SemaphoreType.DMA((2, feats - 1)),
        pltpu.SemaphoreType.DMA((2, feats - 1)),
    ]


def forward_kernel(
    src_ref, local_ref, feat_ref, feat_t_ref, rows_ref, tiles_ref, deg_ref,
    all_feat_ref, all_agg_ref, rows_other_ref,
    ordered, agg_ref, halo_ref, packed, other_t, rows_in, swap_send, swap_recv, mail_send, mail_recv,
    held_feat, send_feat, recv_feat, held_agg, send_agg, recv_agg,
):
    me = lax.axis_index("feat")
    seat = Seat()
    half, place = seat.half, seat.place
    count = feat_t_ref.shape[1]
    blk = halo_ref.shape[1]
    blocks = local_ref.shape[0] // blk
    span = tiles_ref.shape[1] // blk
    seat.enter()
    rows_swap = seat.swap(rows_ref.at[1 - half], rows_in, swap_send.at[0], swap_recv.at[0])
    feat_swap = seat.swap(feat_t_ref, other_t, swap_send.at[1], swap_recv.at[1])
    rows_swap.start()
    feat_swap.start()
    feat_line = LineGather(feat_ref, held_feat, send_feat, recv_feat)
    agg_line = LineGather(agg_ref, held_agg, send_agg, recv_agg)
    feat_line.start(0)

    def mail(turn, step, to, sender):
        z = half if turn == 0 else 1 - half
        return seat.mail(
            packed.at[turn, step], halo_ref.at[2 * sender + z],
            mail_send.at[turn, step], mail_recv.at[z, sender], to,
        )

    def picked(turn, to):
        left = feat_t_ref[...] if turn == 0 else other_t[...]
        wanted = rows_ref[half, pl.ds(to, 1), :] if turn == 0 else rows_in[pl.ds(to, 1), :]
        return jnp.dot(left, one_hot(wanted, count), preferred_element_type=F32).astype(BF)

    def post(turn):
        def act(step, to):
            packed[turn, step] = picked(turn, to)
            mail(turn, step, to, place).start()

        seat.for_mates(act)
        halo_ref[2 * place + (half if turn == 0 else 1 - half)] = picked(turn, place)

    post(0)
    feat_line.arrive(0)
    feat_line.start(1)
    rows_swap.wait()
    feat_swap.wait()
    post(1)
    held_feat[me] = feat_ref[...]
    rows_other_ref[...] = rows_in[...]
    for step in range(1, feat_line.last):
        feat_line.arrive(step)
        if step + 1 < feat_line.last:
            feat_line.start(step + 1)
    for turn in range(2):
        seat.for_mates(lambda step, to: mail(turn, step, to, to).wait_recv())

    def body(b, carry):
        for t in range(span):
            ordered[:, t * blk:(t + 1) * blk] = halo_ref[src_ref[b * span + t]]
        rows = pl.ds(pl.multiple_of(b * blk, blk), blk)
        sums = lax.dot_general(tiles_ref[rows, :], ordered[...], NT, preferred_element_type=F32)
        sums += jnp.dot(local_ref[rows, :], feat_ref[...], preferred_element_type=F32)
        agg_ref[rows, :] = (sums / deg_ref[rows, :]).astype(BF)
        return carry

    lax.fori_loop(0, blocks, body, 0)
    agg_line.start(0)
    held_agg[me] = agg_ref[...]
    for k in range(held_feat.shape[0]):
        all_feat_ref[k] = held_feat[k]
    run_lines([agg_line])
    feat_line.finish()
    for turn in range(2):
        seat.for_mates(lambda step, to: mail(turn, step, to, place).wait_send())
    for k in range(held_agg.shape[0]):
        all_agg_ref[k] = held_agg[k]


def back_kernel(src_ref, scaled_t_ref, tiles_ref, back_ref):
    blk = back_ref.shape[1]
    blocks = scaled_t_ref.shape[1] // blk
    span = tiles_ref.shape[1] // blk
    for b in range(blocks):
        left = scaled_t_ref[:, b * blk:(b + 1) * blk]
        terms = jnp.dot(
            left, tiles_ref[b * blk:(b + 1) * blk, :], preferred_element_type=F32
        ).astype(BF)
        for t in range(span):
            back_ref[src_ref[b * span + t]] = terms[:, t * blk:(t + 1) * blk]


def backward_kernel(
    rows_ref, rows_other_ref, back_ref, scaled_t_ref, local_ref, grad_t_ref, w_ref, share_ref,
    grad_in_ref, grad_w_ref,
    arrived, shares, w_mine, w_in, total, other_ref, landed_ref, neigh_ref, terms, came, went,
    swap_send, swap_recv, mail_send, mail_recv, line_send, line_recv,
):
    me = lax.axis_index("feat")
    last = lax.axis_size("feat") - 1
    seat = Seat()
    half, place = seat.half, seat.place
    count = local_ref.shape[1]
    seat.enter()

    def mail(turn, step, to, sender):
        if turn == 2:
            return seat.mail(
                share_ref.at[to], shares.at[sender],
                mail_send.at[2, step], mail_recv.at[2, sender], to,
            )
        z = 1 - half if turn == 0 else half
        return seat.mail(
            back_ref.at[2 * to + z], arrived.at[2 * sender + z],
            mail_send.at[turn, step], mail_recv.at[turn, sender], to,
        )

    for turn in range(3):
        seat.for_mates(lambda step, to: mail(turn, step, to, place).start())
    arrived[2 * place] = back_ref[2 * place]
    arrived[2 * place + 1] = back_ref[2 * place + 1]
    shares[place] = share_ref[place]
    for k in range(last + 1):
        terms[k] = jnp.dot(w_ref[0, k], grad_t_ref[...], preferred_element_type=F32)

    def unpack(turn):
        z = 1 - half if turn == 0 else half
        seat.for_mates(lambda step, to: mail(turn, step, to, to).wait_recv())

        def rows(j):
            return rows_ref[half, pl.ds(j, 1), :] if turn == 1 else rows_other_ref[pl.ds(j, 1), :]

        def body(i, carry):
            j = 2 * i
            left = jnp.concatenate([arrived[2 * j + z], arrived[2 * j + 2 + z]], axis=1)
            right = jnp.concatenate(
                [one_hot(rows(j), count), one_hot(rows(j + 1), count)], axis=1
            )
            total[...] += lax.dot_general(left, right, NT, preferred_element_type=F32)
            return carry

        lax.fori_loop(0, seat.mates // 2, body, 0, unroll=2)

    total[...] = jnp.zeros_like(total)
    unpack(0)
    other_ref[...] = total[...].astype(BF)
    swap = seat.swap(other_ref, landed_ref, swap_send.at[0], swap_recv.at[0])
    swap.start()
    total[...] = jnp.dot(scaled_t_ref[...], local_ref[...], preferred_element_type=F32)
    unpack(1)
    swap.wait()
    neigh_ref[...] = (total[...] + landed_ref[...].astype(F32)).astype(BF)

    def hop(way, tick):
        target = jnp.clip(me + 1 if way == 0 else me - 1, 0, last)
        return pltpu.make_async_remote_copy(
            src_ref=went.at[way, tick], dst_ref=came.at[way, tick],
            send_sem=line_send.at[way, tick], recv_sem=line_recv.at[way, tick],
            device_id={"feat": target}, device_id_type=pl.DeviceIdType.MESH,
        )

    def rank(way):
        return me if way == 0 else last - me

    def term(k):
        return terms[k] + jnp.dot(w_ref[1, k], neigh_ref[...], preferred_element_type=F32)

    def sends(way, tick):
        return jnp.logical_and(rank(way) <= tick, rank(way) < last)

    for tick in range(last):
        for way in range(2):
            k = jnp.clip(last - tick + me if way == 0 else tick - last + me, 0, last)

            if tick > 0:

                @pl.when(jnp.logical_and(rank(way) <= tick, rank(way) > 0))
                def _():
                    hop(way, tick - 1).wait_recv()

                @pl.when(jnp.logical_and(sends(way, tick), rank(way) > 0))
                def _():
                    went[way, tick] = (term(k) + came[way, tick - 1].astype(F32)).astype(BF)

            @pl.when(rank(way) == 0)
            def _():
                went[way, tick] = term(k).astype(BF)

            @pl.when(sends(way, tick))
            def _():
                hop(way, tick).start()

        if tick == 1:
            seat.for_mates(lambda step, to: mail(2, step, to, to).wait_recv())
            summed = jnp.sum(shares[...].astype(F32), axis=0)
            w_mine[...] = summed.reshape(w_mine.shape)
            w_swap = seat.swap(w_mine.at[1 - half], w_in, swap_send.at[1], swap_recv.at[1])
            w_swap.start()
    total[...] = term(me)
    for way in range(2):

        @pl.when(rank(way) > 0)
        def _():
            hop(way, last - 1).wait_recv()
            total[...] += came[way, last - 1].astype(F32)

    grad_in_ref[...] = total[...].astype(BF)
    w_swap.wait()
    grad_w_ref[...] = w_mine[half] + w_in[...]
    for tick in range(last):
        for way in range(2):

            @pl.when(sends(way, tick))
            def _():
                hop(way, tick).wait_send()

    for turn in range(3):
        seat.for_mates(lambda step, to: mail(turn, step, to, place).wait_send())


def per_device(features, weights, send_rows, remote_src, local_adj, remote_adj, degree, cotangent):
    np_rows, width = features.shape
    feats = lax.axis_size("feat")
    doms = lax.axis_size("dom")
    blk = remote_adj.shape[2]
    span = remote_adj.shape[1] * blk
    mates = doms // 2
    rows = send_rows[0].reshape(doms // (2 * PAIR), 2, PAIR, blk).transpose(1, 0, 2, 3)
    rows = rows.reshape(2, mates, blk)
    w_pair = weights.reshape(2, feats, width, width)

    src = remote_src[0]
    slots = ((src // (2 * PAIR)) * PAIR + src % PAIR) * 2 + (src // PAIR) % 2
    tiles = remote_adj.reshape(np_rows, span)
    deg = jnp.broadcast_to(degree.astype(F32)[:, None], (np_rows, width))
    gathered_feat, gathered_agg, rows_other = pl.pallas_call(
        forward_kernel,
        out_shape=(jax.ShapeDtypeStruct((feats, np_rows, width), BF),) * 2
        + (jax.ShapeDtypeStruct((mates, blk), jnp.int32),),
        in_specs=[smem()] + [vmem()] * 6,
        out_specs=(vmem(), vmem(), vmem()),
        scratch_shapes=[
            pltpu.VMEM((width, span), BF),
            pltpu.VMEM((np_rows, width), BF),
            pltpu.VMEM((doms, width, blk), BF),
            pltpu.VMEM((2, mates, width, blk), BF),
            pltpu.VMEM((width, np_rows), BF),
            pltpu.VMEM((mates, blk), jnp.int32),
            pltpu.SemaphoreType.DMA((2,)),
            pltpu.SemaphoreType.DMA((2,)),
            pltpu.SemaphoreType.DMA((2, mates)),
            pltpu.SemaphoreType.DMA((2, mates)),
        ]
        + line_scratch(feats, np_rows, width) * 2,
        compiler_params=linked(1),
    )(slots, local_adj, features, features.T, rows, tiles, deg)

    full = width * feats
    preact = jnp.einsum(
        "krf,kfc->rc", gathered_feat, w_pair[0], preferred_element_type=F32
    ) + jnp.einsum("krf,kfc->rc", gathered_agg, w_pair[1], preferred_element_type=F32)
    output = jax.nn.silu(preact).astype(BF)
    sig = jax.nn.sigmoid(preact)
    grad_pre = (cotangent.astype(F32) * sig * (1.0 + preact * (1.0 - sig))).astype(BF)
    scaled = (grad_pre.astype(F32) / deg).astype(BF)
    scaled_t = scaled.T

    back = pl.pallas_call(
        back_kernel,
        out_shape=jax.ShapeDtypeStruct((doms, width, blk), BF),
        in_specs=[smem(), vmem(), vmem()],
        out_specs=vmem(),
        compiler_params=params(),
    )(slots, scaled_t, tiles)

    def weight_terms(left):
        return jnp.einsum("krf,rc->kfc", left, grad_pre, preferred_element_type=F32)

    cut = 2 * full // doms
    share = jnp.stack([weight_terms(gathered_feat), weight_terms(gathered_agg)]).astype(BF)
    share = share.reshape(doms // (2 * PAIR), 2, PAIR, cut, width).transpose(0, 2, 1, 3, 4)
    share = share.reshape(mates, 2 * cut, width)
    last = feats - 1
    grad_input_t, summed = pl.pallas_call(
        backward_kernel,
        out_shape=(
            jax.ShapeDtypeStruct((width, np_rows), BF),
            jax.ShapeDtypeStruct((cut, width), F32),
        ),
        in_specs=[vmem()] * 8,
        out_specs=(vmem(), vmem()),
        scratch_shapes=[
            pltpu.VMEM((doms, width, blk), BF),
            pltpu.VMEM((mates, 2 * cut, width), BF),
            pltpu.VMEM((2, cut, width), F32),
            pltpu.VMEM((cut, width), F32),
            pltpu.VMEM((width, np_rows), F32),
            pltpu.VMEM((width, np_rows), BF),
            pltpu.VMEM((width, np_rows), BF),
            pltpu.VMEM((width, np_rows), BF),
            pltpu.VMEM((feats, width, np_rows), F32),
            pltpu.VMEM((2, last, width, np_rows), BF),
            pltpu.VMEM((2, last, width, np_rows), BF),
            pltpu.SemaphoreType.DMA((2,)),
            pltpu.SemaphoreType.DMA((2,)),
            pltpu.SemaphoreType.DMA((3, mates)),
            pltpu.SemaphoreType.DMA((3, mates)),
            pltpu.SemaphoreType.DMA((2, last)),
            pltpu.SemaphoreType.DMA((2, last)),
        ],
        compiler_params=linked(2),
    )(rows, rows_other, back, scaled_t, local_adj, grad_pre.T, w_pair, share)
    weight_scale = 1.0 / math.sqrt(doms * np_rows)
    return (output, grad_input_t.T, summed * weight_scale)


def solution(mesh):
    in_specs = (
        P("dom", "feat"),
        P(None, "feat"),
        P("dom", None, None),
        P("dom", None),
        P("dom", None),
        P("dom", None, None),
        P("dom"),
        P("dom", "feat"),
    )
    out_specs = (P("dom", "feat"), P("dom", "feat"), P("dom", "feat"))
    return jax.shard_map(
        per_device, mesh=mesh, in_specs=in_specs, out_specs=out_specs, check_vma=False
    )
```

```python
import math

import jax
import jax.numpy as jnp
from jax import lax
from jax.experimental import pallas as pl
from jax.experimental.pallas import tpu as pltpu
from jax.sharding import PartitionSpec as P

BF = jnp.bfloat16
PARTS = 2
F32 = jnp.float32
VMEM_BYTES = 48 * 1024 * 1024
PAIR = 8
NT = (((1,), (1,)), ((), ()))


def vmem():
    return pl.BlockSpec(memory_space=pltpu.VMEM)


def smem():
    return pl.BlockSpec(memory_space=pltpu.SMEM)


def params():
    return pltpu.CompilerParams(vmem_limit_bytes=VMEM_BYTES)


def linked(number):
    return pltpu.CompilerParams(
        vmem_limit_bytes=VMEM_BYTES, collective_id=number, has_side_effects=True
    )


def one_hot(rows, count):
    spots = lax.broadcasted_iota(jnp.int32, (count, rows.shape[1]), 0)
    return jnp.where(spots == rows, 1.0, 0.0).astype(BF)


def signal(place):
    pl.semaphore_signal(
        pltpu.get_barrier_semaphore(), inc=1, device_id=place, device_id_type=pl.DeviceIdType.MESH
    )


class Seat:
    def __init__(self):
        self.dom = lax.axis_index("dom")
        self.mates = lax.axis_size("dom") // 2
        self.half = lax.rem(self.dom // PAIR, 2)
        self.partner = self.dom + PAIR * (1 - 2 * self.half)
        self.place = (self.dom // (2 * PAIR)) * PAIR + lax.rem(self.dom, PAIR)

    def mate(self, step):
        return lax.rem(self.place + step, self.mates)

    def dom_of(self, place):
        return (place // PAIR) * (2 * PAIR) + self.half * PAIR + lax.rem(place, PAIR)

    def enter(self):
        me = lax.axis_index("feat")
        feats = lax.axis_size("feat")
        signal({"feat": lax.rem(me + 1, feats)})
        signal({"feat": lax.rem(me + feats - 1, feats)})
        signal({"dom": self.partner})

        def body(step, carry):
            signal({"dom": self.dom_of(self.mate(step))})
            return carry

        lax.fori_loop(1, self.mates, body, 0)
        pl.semaphore_wait(pltpu.get_barrier_semaphore(), self.mates + 2)

    def swap(self, src, dst, send, recv):
        return pltpu.make_async_remote_copy(
            src_ref=src, dst_ref=dst, send_sem=send, recv_sem=recv,
            device_id={"dom": self.partner}, device_id_type=pl.DeviceIdType.MESH,
        )

    def mail(self, src, dst, send, recv, place):
        return pltpu.make_async_remote_copy(
            src_ref=src, dst_ref=dst, send_sem=send, recv_sem=recv,
            device_id={"dom": self.dom_of(place)}, device_id_type=pl.DeviceIdType.MESH,
        )

    def for_mates(self, act):
        def body(step, carry):
            act(step, self.mate(step))
            return carry

        lax.fori_loop(1, self.mates, body, 0)


class LineGather:
    def __init__(self, own, blocks, send, recv):
        self.own, self.blocks, self.send, self.recv = own, blocks, send, recv
        self.me = lax.axis_index("feat")
        self.last = lax.axis_size("feat") - 1

    def copy(self, way, step, coming=0):
        up = way == 0
        back = step + coming
        source = jnp.clip(self.me - back if up else self.me + back, 0, self.last)
        target = jnp.clip(self.me + 1 if up else self.me - 1, 0, self.last)
        return pltpu.make_async_remote_copy(
            src_ref=self.own if back == 0 else self.blocks.at[source],
            dst_ref=self.blocks.at[source],
            send_sem=self.send.at[way, step],
            recv_sem=self.recv.at[way, step],
            device_id={"feat": target},
            device_id_type=pl.DeviceIdType.MESH,
        )

    def sends(self, way, step):
        if way == 0:
            return jnp.logical_and(self.me >= step, self.me < self.last)
        return jnp.logical_and(self.me <= self.last - step, self.me > 0)

    def gets(self, way, step):
        return self.me > step if way == 0 else self.me < self.last - step

    def start(self, step):
        for way in range(2):

            @pl.when(self.sends(way, step))
            def _():
                self.copy(way, step).start()

    def arrive(self, step):
        for way in range(2):

            @pl.when(self.gets(way, step))
            def _():
                self.copy(way, step, 1).wait_recv()

    def finish(self):
        for step in range(self.last):
            for way in range(2):

                @pl.when(self.sends(way, step))
                def _():
                    self.copy(way, step).wait_send()


def gather_lines(own, held, send, recv):
    rows = held.shape[2]
    return [
        LineGather(own.at[pl.ds(c * rows, rows)], held.at[c], send.at[c], recv.at[c])
        for c in range(PARTS)
    ]


def hand_on(lines, step):
    for line in lines:
        line.arrive(step)
        if step + 1 < line.last:
            line.start(step + 1)


def line_scratch(feats, rows, width):
    return [
        pltpu.VMEM((PARTS, feats, rows // PARTS, width), BF),
        pltpu.SemaphoreType.DMA((PARTS, 2, feats - 1)),
        pltpu.SemaphoreType.DMA((PARTS, 2, feats - 1)),
    ]


def forward_kernel(
    src_ref, local_ref, feat_ref, feat_t_ref, rows_ref, tiles_ref, deg_ref,
    all_feat_ref, all_agg_ref, rows_other_ref,
    ordered, agg_ref, halo_ref, packed, other_t, rows_in, swap_send, swap_recv, mail_send, mail_recv,
    held_feat, send_feat, recv_feat, held_agg, send_agg, recv_agg,
):
    me = lax.axis_index("feat")
    seat = Seat()
    half, place = seat.half, seat.place
    count = feat_t_ref.shape[1]
    blk = halo_ref.shape[1]
    blocks = local_ref.shape[0] // blk
    span = tiles_ref.shape[1] // blk
    seat.enter()
    rows_swap = seat.swap(rows_ref.at[1 - half], rows_in, swap_send.at[0], swap_recv.at[0])
    feat_swap = seat.swap(feat_t_ref, other_t, swap_send.at[1], swap_recv.at[1])
    rows_swap.start()
    feat_swap.start()
    feat_lines = gather_lines(feat_ref, held_feat, send_feat, recv_feat)
    agg_lines = gather_lines(agg_ref, held_agg, send_agg, recv_agg)
    last = feat_lines[0].last
    rows_part = held_feat.shape[2]
    early = last - 2

    def mail(turn, step, to, sender):
        z = half if turn == 0 else 1 - half
        return seat.mail(
            packed.at[turn, step], halo_ref.at[2 * sender + z],
            mail_send.at[turn, step], mail_recv.at[z, sender], to,
        )

    def picked(turn, to):
        left = feat_t_ref[...] if turn == 0 else other_t[...]
        wanted = rows_ref[half, pl.ds(to, 1), :] if turn == 0 else rows_in[pl.ds(to, 1), :]
        return jnp.dot(left, one_hot(wanted, count), preferred_element_type=F32).astype(BF)

    def post(turn):
        def act(step, to):
            packed[turn, step] = picked(turn, to)
            mail(turn, step, to, place).start()

        seat.for_mates(act)
        halo_ref[2 * place + (half if turn == 0 else 1 - half)] = picked(turn, place)

    post(0)
    rows_swap.wait()
    feat_swap.wait()
    for line in feat_lines:
        line.start(0)
    post(1)
    for c in range(PARTS):
        held_feat[c, me] = feat_ref[c * rows_part:(c + 1) * rows_part, :]
    rows_other_ref[...] = rows_in[...]
    for step in range(early):
        hand_on(feat_lines, step)
    for turn in range(2):
        seat.for_mates(lambda step, to: mail(turn, step, to, to).wait_recv())

    def body(b, carry):
        for t in range(span):
            ordered[:, t * blk:(t + 1) * blk] = halo_ref[src_ref[b * span + t]]
        rows = pl.ds(pl.multiple_of(b * blk, blk), blk)
        sums = lax.dot_general(tiles_ref[rows, :], ordered[...], NT, preferred_element_type=F32)
        sums += jnp.dot(local_ref[rows, :], feat_ref[...], preferred_element_type=F32)
        agg_ref[rows, :] = (sums / deg_ref[rows, :]).astype(BF)
        return carry

    for c in range(PARTS):
        lax.fori_loop(c * blocks // PARTS, (c + 1) * blocks // PARTS, body, 0)
        agg_lines[c].start(0)
    for c in range(PARTS):
        held_agg[c, me] = agg_ref[c * rows_part:(c + 1) * rows_part, :]
    for step in range(early, last):
        hand_on(feat_lines, step)
    for step in range(last):
        hand_on(agg_lines, step)
        if step == 0:
            for c in range(PARTS):
                for k in range(held_feat.shape[1]):
                    all_feat_ref[k, c * rows_part:(c + 1) * rows_part, :] = held_feat[c, k]
    for line in feat_lines + agg_lines:
        line.finish()
    for turn in range(2):
        seat.for_mates(lambda step, to: mail(turn, step, to, place).wait_send())
    for c in range(PARTS):
        for k in range(held_agg.shape[1]):
            all_agg_ref[k, c * rows_part:(c + 1) * rows_part, :] = held_agg[c, k]


def back_kernel(src_ref, scaled_t_ref, tiles_ref, back_ref):
    blk = back_ref.shape[1]
    blocks = scaled_t_ref.shape[1] // blk
    span = tiles_ref.shape[1] // blk
    for b in range(blocks):
        left = scaled_t_ref[:, b * blk:(b + 1) * blk]
        terms = jnp.dot(
            left, tiles_ref[b * blk:(b + 1) * blk, :], preferred_element_type=F32
        ).astype(BF)
        for t in range(span):
            back_ref[src_ref[b * span + t]] = terms[:, t * blk:(t + 1) * blk]


def backward_kernel(
    rows_ref, rows_other_ref, back_ref, scaled_t_ref, local_ref, grad_t_ref, w_ref, share_ref,
    grad_in_ref, grad_w_ref,
    arrived, shares, w_mine, w_in, total, other_ref, landed_ref, neigh_ref, terms, came, went,
    swap_send, swap_recv, mail_send, mail_recv, line_send, line_recv,
):
    me = lax.axis_index("feat")
    last = lax.axis_size("feat") - 1
    seat = Seat()
    half, place = seat.half, seat.place
    count = local_ref.shape[1]
    seat.enter()

    def mail(turn, step, to, sender):
        if turn == 2:
            return seat.mail(
                share_ref.at[to], shares.at[sender],
                mail_send.at[2, step], mail_recv.at[2, sender], to,
            )
        z = 1 - half if turn == 0 else half
        return seat.mail(
            back_ref.at[2 * to + z], arrived.at[2 * sender + z],
            mail_send.at[turn, step], mail_recv.at[turn, sender], to,
        )

    for turn in range(3):
        seat.for_mates(lambda step, to: mail(turn, step, to, place).start())
    arrived[2 * place] = back_ref[2 * place]
    arrived[2 * place + 1] = back_ref[2 * place + 1]
    shares[place] = share_ref[place]
    for k in range(last + 1):
        terms[k] = jnp.dot(w_ref[0, k], grad_t_ref[...], preferred_element_type=F32)

    def unpack(turn):
        z = 1 - half if turn == 0 else half
        seat.for_mates(lambda step, to: mail(turn, step, to, to).wait_recv())

        def rows(j):
            return rows_ref[half, pl.ds(j, 1), :] if turn == 1 else rows_other_ref[pl.ds(j, 1), :]

        def body(i, carry):
            j = 2 * i
            left = jnp.concatenate([arrived[2 * j + z], arrived[2 * j + 2 + z]], axis=1)
            right = jnp.concatenate(
                [one_hot(rows(j), count), one_hot(rows(j + 1), count)], axis=1
            )
            total[...] += lax.dot_general(left, right, NT, preferred_element_type=F32)
            return carry

        lax.fori_loop(0, seat.mates // 2, body, 0, unroll=2)

    total[...] = jnp.zeros_like(total)
    unpack(0)
    other_ref[...] = total[...].astype(BF)
    swap = seat.swap(other_ref, landed_ref, swap_send.at[0], swap_recv.at[0])
    swap.start()
    total[...] = jnp.dot(scaled_t_ref[...], local_ref[...], preferred_element_type=F32)
    unpack(1)
    swap.wait()
    neigh_ref[...] = (total[...] + landed_ref[...].astype(F32)).astype(BF)

    part = came.shape[4]

    def hop(c, way, tick):
        target = jnp.clip(me + 1 if way == 0 else me - 1, 0, last)
        return pltpu.make_async_remote_copy(
            src_ref=went.at[c, way, tick], dst_ref=came.at[c, way, tick],
            send_sem=line_send.at[c, way, tick], recv_sem=line_recv.at[c, way, tick],
            device_id={"feat": target}, device_id_type=pl.DeviceIdType.MESH,
        )

    def rank(way):
        return me if way == 0 else last - me

    def term(k):
        return terms[k] + jnp.dot(w_ref[1, k], neigh_ref[...], preferred_element_type=F32)

    def sends(way, tick):
        return jnp.logical_and(rank(way) <= tick, rank(way) < last)

    for tick in range(last):
        blocks = [
            jnp.clip(last - tick + me if way == 0 else tick - last + me, 0, last)
            for way in range(2)
        ]
        for way in range(2):

            @pl.when(sends(way, tick))
            def _():
                terms[blocks[way]] = term(blocks[way])

        for c in range(PARTS):
            for way in range(2):
                lanes = slice(c * part, (c + 1) * part)

                if tick > 0:

                    @pl.when(jnp.logical_and(rank(way) <= tick, rank(way) > 0))
                    def _():
                        hop(c, way, tick - 1).wait_recv()

                    @pl.when(jnp.logical_and(sends(way, tick), rank(way) > 0))
                    def _():
                        went[c, way, tick] = (
                            terms[blocks[way], :, lanes] + came[c, way, tick - 1].astype(F32)
                        ).astype(BF)

                @pl.when(rank(way) == 0)
                def _():
                    went[c, way, tick] = terms[blocks[way], :, lanes].astype(BF)

                @pl.when(sends(way, tick))
                def _():
                    hop(c, way, tick).start()

        if tick == 1:
            seat.for_mates(lambda step, to: mail(2, step, to, to).wait_recv())
            summed = jnp.sum(shares[...].astype(F32), axis=0)
            w_mine[...] = summed.reshape(w_mine.shape)
            w_swap = seat.swap(w_mine.at[1 - half], w_in, swap_send.at[1], swap_recv.at[1])
            w_swap.start()
    total[...] = term(me)
    for c in range(PARTS):
        for way in range(2):

            @pl.when(rank(way) > 0)
            def _():
                hop(c, way, last - 1).wait_recv()
                total[:, c * part:(c + 1) * part] += came[c, way, last - 1].astype(F32)

    grad_in_ref[...] = total[...].astype(BF)
    w_swap.wait()
    grad_w_ref[...] = w_mine[half] + w_in[...]
    for tick in range(last):
        for c in range(PARTS):
            for way in range(2):

                @pl.when(sends(way, tick))
                def _():
                    hop(c, way, tick).wait_send()

    for turn in range(3):
        seat.for_mates(lambda step, to: mail(turn, step, to, place).wait_send())


def per_device(features, weights, send_rows, remote_src, local_adj, remote_adj, degree, cotangent):
    np_rows, width = features.shape
    feats = lax.axis_size("feat")
    doms = lax.axis_size("dom")
    blk = remote_adj.shape[2]
    span = remote_adj.shape[1] * blk
    mates = doms // 2
    rows = send_rows[0].reshape(doms // (2 * PAIR), 2, PAIR, blk).transpose(1, 0, 2, 3)
    rows = rows.reshape(2, mates, blk)
    w_pair = weights.reshape(2, feats, width, width)

    src = remote_src[0]
    slots = ((src // (2 * PAIR)) * PAIR + src % PAIR) * 2 + (src // PAIR) % 2
    tiles = remote_adj.reshape(np_rows, span)
    deg = jnp.broadcast_to(degree.astype(F32)[:, None], (np_rows, width))
    gathered_feat, gathered_agg, rows_other = pl.pallas_call(
        forward_kernel,
        out_shape=(jax.ShapeDtypeStruct((feats, np_rows, width), BF),) * 2
        + (jax.ShapeDtypeStruct((mates, blk), jnp.int32),),
        in_specs=[smem()] + [vmem()] * 6,
        out_specs=(vmem(), vmem(), vmem()),
        scratch_shapes=[
            pltpu.VMEM((width, span), BF),
            pltpu.VMEM((np_rows, width), BF),
            pltpu.VMEM((doms, width, blk), BF),
            pltpu.VMEM((2, mates, width, blk), BF),
            pltpu.VMEM((width, np_rows), BF),
            pltpu.VMEM((mates, blk), jnp.int32),
            pltpu.SemaphoreType.DMA((2,)),
            pltpu.SemaphoreType.DMA((2,)),
            pltpu.SemaphoreType.DMA((2, mates)),
            pltpu.SemaphoreType.DMA((2, mates)),
        ]
        + line_scratch(feats, np_rows, width) * 2,
        compiler_params=linked(1),
    )(slots, local_adj, features, features.T, rows, tiles, deg)

    full = width * feats
    preact = jnp.einsum(
        "krf,kfc->rc", gathered_feat, w_pair[0], preferred_element_type=F32
    ) + jnp.einsum("krf,kfc->rc", gathered_agg, w_pair[1], preferred_element_type=F32)
    output = jax.nn.silu(preact).astype(BF)
    sig = jax.nn.sigmoid(preact)
    grad_pre = (cotangent.astype(F32) * sig * (1.0 + preact * (1.0 - sig))).astype(BF)
    scaled = (grad_pre.astype(F32) / deg).astype(BF)
    scaled_t = scaled.T

    back = pl.pallas_call(
        back_kernel,
        out_shape=jax.ShapeDtypeStruct((doms, width, blk), BF),
        in_specs=[smem(), vmem(), vmem()],
        out_specs=vmem(),
        compiler_params=params(),
    )(slots, scaled_t, tiles)

    def weight_terms(left):
        return jnp.einsum("krf,rc->kfc", left, grad_pre, preferred_element_type=F32)

    cut = 2 * full // doms
    share = jnp.stack([weight_terms(gathered_feat), weight_terms(gathered_agg)]).astype(BF)
    share = share.reshape(doms // (2 * PAIR), 2, PAIR, cut, width).transpose(0, 2, 1, 3, 4)
    share = share.reshape(mates, 2 * cut, width)
    last = feats - 1
    grad_input_t, summed = pl.pallas_call(
        backward_kernel,
        out_shape=(
            jax.ShapeDtypeStruct((width, np_rows), BF),
            jax.ShapeDtypeStruct((cut, width), F32),
        ),
        in_specs=[vmem()] * 8,
        out_specs=(vmem(), vmem()),
        scratch_shapes=[
            pltpu.VMEM((doms, width, blk), BF),
            pltpu.VMEM((mates, 2 * cut, width), BF),
            pltpu.VMEM((2, cut, width), F32),
            pltpu.VMEM((cut, width), F32),
            pltpu.VMEM((width, np_rows), F32),
            pltpu.VMEM((width, np_rows), BF),
            pltpu.VMEM((width, np_rows), BF),
            pltpu.VMEM((width, np_rows), BF),
            pltpu.VMEM((feats, width, np_rows), F32),
            pltpu.VMEM((PARTS, 2, last, width, np_rows // PARTS), BF),
            pltpu.VMEM((PARTS, 2, last, width, np_rows // PARTS), BF),
            pltpu.SemaphoreType.DMA((2,)),
            pltpu.SemaphoreType.DMA((2,)),
            pltpu.SemaphoreType.DMA((3, mates)),
            pltpu.SemaphoreType.DMA((3, mates)),
            pltpu.SemaphoreType.DMA((PARTS, 2, last)),
            pltpu.SemaphoreType.DMA((PARTS, 2, last)),
        ],
        compiler_params=linked(2),
    )(rows, rows_other, back, scaled_t, local_adj, grad_pre.T, w_pair, share)
    weight_scale = 1.0 / math.sqrt(doms * np_rows)
    return (output, grad_input_t.T, summed * weight_scale)


def solution(mesh):
    in_specs = (
        P("dom", "feat"),
        P(None, "feat"),
        P("dom", None, None),
        P("dom", None),
        P("dom", None),
        P("dom", None, None),
        P("dom"),
        P("dom", "feat"),
    )
    out_specs = (P("dom", "feat"), P("dom", "feat"), P("dom", "feat"))
    return jax.shard_map(
        per_device, mesh=mesh, in_specs=in_specs, out_specs=out_specs, check_vma=False
    )
```

```python
import math

import jax
import jax.numpy as jnp
from jax import lax
from jax.experimental import pallas as pl
from jax.experimental.pallas import tpu as pltpu
from jax.sharding import PartitionSpec as P

BF = jnp.bfloat16
PARTS = 4
F32 = jnp.float32
VMEM_BYTES = 48 * 1024 * 1024
PAIR = 8
NT = (((1,), (1,)), ((), ()))


def vmem():
    return pl.BlockSpec(memory_space=pltpu.VMEM)


def far():
    return pl.BlockSpec(memory_space=pl.ANY)


def smem():
    return pl.BlockSpec(memory_space=pltpu.SMEM)


def params():
    return pltpu.CompilerParams(vmem_limit_bytes=VMEM_BYTES)


def linked(number):
    return pltpu.CompilerParams(
        vmem_limit_bytes=VMEM_BYTES, collective_id=number, has_side_effects=True
    )


def one_hot(rows, count):
    spots = lax.broadcasted_iota(jnp.int32, (count, rows.shape[1]), 0)
    return jnp.where(spots == rows, 1.0, 0.0).astype(BF)


def signal(place):
    pl.semaphore_signal(
        pltpu.get_barrier_semaphore(), inc=1, device_id=place, device_id_type=pl.DeviceIdType.MESH
    )


class Seat:
    def __init__(self):
        self.dom = lax.axis_index("dom")
        self.mates = lax.axis_size("dom") // 2
        self.half = lax.rem(self.dom // PAIR, 2)
        self.partner = self.dom + PAIR * (1 - 2 * self.half)
        self.place = (self.dom // (2 * PAIR)) * PAIR + lax.rem(self.dom, PAIR)

    def mate(self, step):
        return lax.rem(self.place + step, self.mates)

    def dom_of(self, place):
        return (place // PAIR) * (2 * PAIR) + self.half * PAIR + lax.rem(place, PAIR)

    def enter(self):
        me = lax.axis_index("feat")
        feats = lax.axis_size("feat")
        signal({"feat": lax.rem(me + 1, feats)})
        signal({"feat": lax.rem(me + feats - 1, feats)})
        signal({"dom": self.partner})

        def body(step, carry):
            signal({"dom": self.dom_of(self.mate(step))})
            return carry

        lax.fori_loop(1, self.mates, body, 0)
        pl.semaphore_wait(pltpu.get_barrier_semaphore(), self.mates + 2)

    def swap(self, src, dst, send, recv):
        return pltpu.make_async_remote_copy(
            src_ref=src, dst_ref=dst, send_sem=send, recv_sem=recv,
            device_id={"dom": self.partner}, device_id_type=pl.DeviceIdType.MESH,
        )

    def mail(self, src, dst, send, recv, place):
        return pltpu.make_async_remote_copy(
            src_ref=src, dst_ref=dst, send_sem=send, recv_sem=recv,
            device_id={"dom": self.dom_of(place)}, device_id_type=pl.DeviceIdType.MESH,
        )

    def for_mates(self, act):
        def body(step, carry):
            act(step, self.mate(step))
            return carry

        lax.fori_loop(1, self.mates, body, 0)


class LineGather:
    def __init__(self, own, blocks, send, recv):
        self.own, self.blocks, self.send, self.recv = own, blocks, send, recv
        self.me = lax.axis_index("feat")
        self.last = lax.axis_size("feat") - 1

    def copy(self, way, step, coming=0):
        up = way == 0
        back = step + coming
        source = jnp.clip(self.me - back if up else self.me + back, 0, self.last)
        target = jnp.clip(self.me + 1 if up else self.me - 1, 0, self.last)
        return pltpu.make_async_remote_copy(
            src_ref=self.own if back == 0 else self.blocks.at[source],
            dst_ref=self.blocks.at[source],
            send_sem=self.send.at[way, step],
            recv_sem=self.recv.at[way, step],
            device_id={"feat": target},
            device_id_type=pl.DeviceIdType.MESH,
        )

    def sends(self, way, step):
        if way == 0:
            return jnp.logical_and(self.me >= step, self.me < self.last)
        return jnp.logical_and(self.me <= self.last - step, self.me > 0)

    def gets(self, way, step):
        return self.me > step if way == 0 else self.me < self.last - step

    def start(self, step):
        for way in range(2):

            @pl.when(self.sends(way, step))
            def _():
                self.copy(way, step).start()

    def arrive(self, step):
        for way in range(2):

            @pl.when(self.gets(way, step))
            def _():
                self.copy(way, step, 1).wait_recv()

    def finish(self):
        for step in range(self.last):
            for way in range(2):

                @pl.when(self.sends(way, step))
                def _():
                    self.copy(way, step).wait_send()


def gather_lines(own, held, send, recv):
    rows = held.shape[2]
    return [
        LineGather(own.at[pl.ds(c * rows, rows)], held.at[c], send.at[c], recv.at[c])
        for c in range(PARTS)
    ]


def hand_on(lines, step):
    for line in lines:
        line.arrive(step)
        if step + 1 < line.last:
            line.start(step + 1)


def line_scratch(feats, rows, width):
    return [
        pltpu.VMEM((PARTS, feats, rows // PARTS, width), BF),
        pltpu.SemaphoreType.DMA((PARTS, 2, feats - 1)),
        pltpu.SemaphoreType.DMA((PARTS, 2, feats - 1)),
    ]


def forward_kernel(
    src_ref, local_far, feat_ref, feat_t_ref, rows_ref, tiles_far, deg_far,
    all_feat_ref, all_agg_ref, rows_other_ref,
    local_ref, tiles_ref, deg_ref, near_sem, ordered, agg_ref, halo_ref, packed, other_t, rows_in, swap_send, swap_recv, mail_send, mail_recv,
    held_feat, send_feat, recv_feat, held_agg, send_agg, recv_agg,
):
    me = lax.axis_index("feat")
    seat = Seat()
    half, place = seat.half, seat.place
    count = feat_t_ref.shape[1]
    blk = halo_ref.shape[1]
    blocks = local_ref.shape[0] // blk
    span = tiles_ref.shape[1] // blk
    seat.enter()
    rows_swap = seat.swap(rows_ref.at[1 - half], rows_in, swap_send.at[0], swap_recv.at[0])
    feat_swap = seat.swap(feat_t_ref, other_t, swap_send.at[1], swap_recv.at[1])
    fetches = [
        pltpu.make_async_copy(far, near, near_sem.at[i])
        for i, (far, near) in enumerate(
            [(local_far, local_ref), (tiles_far, tiles_ref), (deg_far, deg_ref)]
        )
    ]
    rows_swap.start()
    feat_swap.start()
    for fetch in fetches:
        fetch.start()
    feat_lines = gather_lines(feat_ref, held_feat, send_feat, recv_feat)
    agg_lines = gather_lines(agg_ref, held_agg, send_agg, recv_agg)
    last = feat_lines[0].last
    rows_part = held_feat.shape[2]
    early = last - 2

    def mail(turn, step, to, sender):
        z = half if turn == 0 else 1 - half
        return seat.mail(
            packed.at[turn, step], halo_ref.at[2 * sender + z],
            mail_send.at[turn, step], mail_recv.at[z, sender], to,
        )

    def picked(turn, to):
        left = feat_t_ref[...] if turn == 0 else other_t[...]
        wanted = rows_ref[half, pl.ds(to, 1), :] if turn == 0 else rows_in[pl.ds(to, 1), :]
        return jnp.dot(left, one_hot(wanted, count), preferred_element_type=F32).astype(BF)

    def post(turn):
        def act(step, to):
            packed[turn, step] = picked(turn, to)
            mail(turn, step, to, place).start()

        seat.for_mates(act)
        halo_ref[2 * place + (half if turn == 0 else 1 - half)] = picked(turn, place)

    post(0)
    rows_swap.wait()
    feat_swap.wait()
    for line in feat_lines:
        line.start(0)
    post(1)
    for c in range(PARTS):
        held_feat[c, me] = feat_ref[c * rows_part:(c + 1) * rows_part, :]
    rows_other_ref[...] = rows_in[...]
    for step in range(early):
        hand_on(feat_lines, step)
    for turn in range(2):
        seat.for_mates(lambda step, to: mail(turn, step, to, to).wait_recv())

    for fetch in fetches:
        fetch.wait()

    def body(b, carry):
        for t in range(span):
            ordered[:, t * blk:(t + 1) * blk] = halo_ref[src_ref[b * span + t]]
        rows = pl.ds(pl.multiple_of(b * blk, blk), blk)
        sums = lax.dot_general(tiles_ref[rows, :], ordered[...], NT, preferred_element_type=F32)
        sums += jnp.dot(local_ref[rows, :], feat_ref[...], preferred_element_type=F32)
        agg_ref[rows, :] = (sums / deg_ref[rows, :]).astype(BF)
        return carry

    for c in range(PARTS):
        lax.fori_loop(c * blocks // PARTS, (c + 1) * blocks // PARTS, body, 0)
        agg_lines[c].start(0)
    for c in range(PARTS):
        held_agg[c, me] = agg_ref[c * rows_part:(c + 1) * rows_part, :]
    for step in range(early, last):
        hand_on(feat_lines, step)
    for step in range(last):
        hand_on(agg_lines, step)
        if step == 0:
            for c in range(PARTS):
                for k in range(held_feat.shape[1]):
                    all_feat_ref[k, c * rows_part:(c + 1) * rows_part, :] = held_feat[c, k]
    for line in feat_lines + agg_lines:
        line.finish()
    for turn in range(2):
        seat.for_mates(lambda step, to: mail(turn, step, to, place).wait_send())
    for c in range(PARTS):
        for k in range(held_agg.shape[1]):
            all_agg_ref[k, c * rows_part:(c + 1) * rows_part, :] = held_agg[c, k]


def back_kernel(src_ref, scaled_t_ref, tiles_ref, back_ref):
    blk = back_ref.shape[1]
    blocks = scaled_t_ref.shape[1] // blk
    span = tiles_ref.shape[1] // blk
    for b in range(blocks):
        left = scaled_t_ref[:, b * blk:(b + 1) * blk]
        terms = jnp.dot(
            left, tiles_ref[b * blk:(b + 1) * blk, :], preferred_element_type=F32
        ).astype(BF)
        for t in range(span):
            back_ref[src_ref[b * span + t]] = terms[:, t * blk:(t + 1) * blk]


def backward_kernel(
    rows_ref, rows_other_ref, back_ref, scaled_t_ref, local_ref, grad_t_ref, w_ref, share_ref,
    grad_in_ref, grad_w_ref,
    arrived, shares, w_mine, w_in, total, other_ref, landed_ref, neigh_ref, terms, came, went,
    swap_send, swap_recv, mail_send, mail_recv, line_send, line_recv,
):
    me = lax.axis_index("feat")
    last = lax.axis_size("feat") - 1
    seat = Seat()
    half, place = seat.half, seat.place
    count = local_ref.shape[1]
    seat.enter()

    def mail(turn, step, to, sender):
        if turn == 2:
            return seat.mail(
                share_ref.at[to], shares.at[sender],
                mail_send.at[2, step], mail_recv.at[2, sender], to,
            )
        z = 1 - half if turn == 0 else half
        return seat.mail(
            back_ref.at[2 * to + z], arrived.at[2 * sender + z],
            mail_send.at[turn, step], mail_recv.at[turn, sender], to,
        )

    for turn in range(3):
        seat.for_mates(lambda step, to: mail(turn, step, to, place).start())
    arrived[2 * place] = back_ref[2 * place]
    arrived[2 * place + 1] = back_ref[2 * place + 1]
    shares[place] = share_ref[place]
    for k in range(last + 1):
        terms[k] = jnp.dot(w_ref[0, k], grad_t_ref[...], preferred_element_type=F32)

    def unpack(turn):
        z = 1 - half if turn == 0 else half
        seat.for_mates(lambda step, to: mail(turn, step, to, to).wait_recv())

        def rows(j):
            return rows_ref[half, pl.ds(j, 1), :] if turn == 1 else rows_other_ref[pl.ds(j, 1), :]

        def body(i, carry):
            j = 2 * i
            left = jnp.concatenate([arrived[2 * j + z], arrived[2 * j + 2 + z]], axis=1)
            right = jnp.concatenate(
                [one_hot(rows(j), count), one_hot(rows(j + 1), count)], axis=1
            )
            total[...] += lax.dot_general(left, right, NT, preferred_element_type=F32)
            return carry

        lax.fori_loop(0, seat.mates // 2, body, 0, unroll=2)

    total[...] = jnp.zeros_like(total)
    unpack(0)
    other_ref[...] = total[...].astype(BF)
    swap = seat.swap(other_ref, landed_ref, swap_send.at[0], swap_recv.at[0])
    swap.start()
    total[...] = jnp.dot(scaled_t_ref[...], local_ref[...], preferred_element_type=F32)
    unpack(1)
    swap.wait()
    neigh_ref[...] = (total[...] + landed_ref[...].astype(F32)).astype(BF)

    part = came.shape[4]

    def hop(c, way, tick):
        target = jnp.clip(me + 1 if way == 0 else me - 1, 0, last)
        return pltpu.make_async_remote_copy(
            src_ref=went.at[c, way, tick], dst_ref=came.at[c, way, tick],
            send_sem=line_send.at[c, way, tick], recv_sem=line_recv.at[c, way, tick],
            device_id={"feat": target}, device_id_type=pl.DeviceIdType.MESH,
        )

    def rank(way):
        return me if way == 0 else last - me

    def term(k):
        return terms[k] + jnp.dot(w_ref[1, k], neigh_ref[...], preferred_element_type=F32)

    def sends(way, tick):
        return jnp.logical_and(rank(way) <= tick, rank(way) < last)

    for tick in range(last):
        blocks = [
            jnp.clip(last - tick + me if way == 0 else tick - last + me, 0, last)
            for way in range(2)
        ]
        for way in range(2):

            @pl.when(sends(way, tick))
            def _():
                terms[blocks[way]] = term(blocks[way])

        for c in range(PARTS):
            for way in range(2):
                lanes = slice(c * part, (c + 1) * part)

                if tick > 0:

                    @pl.when(jnp.logical_and(rank(way) <= tick, rank(way) > 0))
                    def _():
                        hop(c, way, tick - 1).wait_recv()

                    @pl.when(jnp.logical_and(sends(way, tick), rank(way) > 0))
                    def _():
                        went[c, way, tick] = (
                            terms[blocks[way], :, lanes] + came[c, way, tick - 1].astype(F32)
                        ).astype(BF)

                @pl.when(rank(way) == 0)
                def _():
                    went[c, way, tick] = terms[blocks[way], :, lanes].astype(BF)

                @pl.when(sends(way, tick))
                def _():
                    hop(c, way, tick).start()

        if tick == 1:
            seat.for_mates(lambda step, to: mail(2, step, to, to).wait_recv())
            summed = jnp.sum(shares[...].astype(F32), axis=0)
            w_mine[...] = summed.reshape(w_mine.shape)
            w_swap = seat.swap(w_mine.at[1 - half], w_in, swap_send.at[1], swap_recv.at[1])
            w_swap.start()
    total[...] = term(me)
    for c in range(PARTS):
        for way in range(2):

            @pl.when(rank(way) > 0)
            def _():
                hop(c, way, last - 1).wait_recv()
                total[:, c * part:(c + 1) * part] += came[c, way, last - 1].astype(F32)

    grad_in_ref[...] = total[...].astype(BF)
    w_swap.wait()
    grad_w_ref[...] = w_mine[half] + w_in[...]
    for tick in range(last):
        for c in range(PARTS):
            for way in range(2):

                @pl.when(sends(way, tick))
                def _():
                    hop(c, way, tick).wait_send()

    for turn in range(3):
        seat.for_mates(lambda step, to: mail(turn, step, to, place).wait_send())


def per_device(features, weights, send_rows, remote_src, local_adj, remote_adj, degree, cotangent):
    np_rows, width = features.shape
    feats = lax.axis_size("feat")
    doms = lax.axis_size("dom")
    blk = remote_adj.shape[2]
    span = remote_adj.shape[1] * blk
    mates = doms // 2
    rows = send_rows[0].reshape(doms // (2 * PAIR), 2, PAIR, blk).transpose(1, 0, 2, 3)
    rows = rows.reshape(2, mates, blk)
    w_pair = weights.reshape(2, feats, width, width)

    src = remote_src[0]
    slots = ((src // (2 * PAIR)) * PAIR + src % PAIR) * 2 + (src // PAIR) % 2
    tiles = remote_adj.reshape(np_rows, span)
    deg = jnp.broadcast_to(degree.astype(F32)[:, None], (np_rows, width))
    gathered_feat, gathered_agg, rows_other = pl.pallas_call(
        forward_kernel,
        out_shape=(jax.ShapeDtypeStruct((feats, np_rows, width), BF),) * 2
        + (jax.ShapeDtypeStruct((mates, blk), jnp.int32),),
        in_specs=[smem(), far(), vmem(), vmem(), vmem(), far(), far()],
        out_specs=(vmem(), vmem(), vmem()),
        scratch_shapes=[
            pltpu.VMEM(local_adj.shape, BF),
            pltpu.VMEM(tiles.shape, BF),
            pltpu.VMEM(deg.shape, F32),
            pltpu.SemaphoreType.DMA((3,)),
            pltpu.VMEM((width, span), BF),
            pltpu.VMEM((np_rows, width), BF),
            pltpu.VMEM((doms, width, blk), BF),
            pltpu.VMEM((2, mates, width, blk), BF),
            pltpu.VMEM((width, np_rows), BF),
            pltpu.VMEM((mates, blk), jnp.int32),
            pltpu.SemaphoreType.DMA((2,)),
            pltpu.SemaphoreType.DMA((2,)),
            pltpu.SemaphoreType.DMA((2, mates)),
            pltpu.SemaphoreType.DMA((2, mates)),
        ]
        + line_scratch(feats, np_rows, width) * 2,
        compiler_params=linked(1),
    )(slots, local_adj, features, features.T, rows, tiles, deg)

    full = width * feats
    preact = jnp.einsum(
        "krf,kfc->rc", gathered_feat, w_pair[0], preferred_element_type=F32
    ) + jnp.einsum("krf,kfc->rc", gathered_agg, w_pair[1], preferred_element_type=F32)
    output = jax.nn.silu(preact).astype(BF)
    sig = jax.nn.sigmoid(preact)
    grad_pre = (cotangent.astype(F32) * sig * (1.0 + preact * (1.0 - sig))).astype(BF)
    scaled = (grad_pre.astype(F32) / deg).astype(BF)
    scaled_t = scaled.T

    back = pl.pallas_call(
        back_kernel,
        out_shape=jax.ShapeDtypeStruct((doms, width, blk), BF),
        in_specs=[smem(), vmem(), vmem()],
        out_specs=vmem(),
        compiler_params=params(),
    )(slots, scaled_t, tiles)

    def weight_terms(left):
        return jnp.einsum("krf,rc->kfc", left, grad_pre, preferred_element_type=F32)

    cut = 2 * full // doms
    share = jnp.stack([weight_terms(gathered_feat), weight_terms(gathered_agg)]).astype(BF)
    share = share.reshape(doms // (2 * PAIR), 2, PAIR, cut, width).transpose(0, 2, 1, 3, 4)
    share = share.reshape(mates, 2 * cut, width)
    last = feats - 1
    grad_input_t, summed = pl.pallas_call(
        backward_kernel,
        out_shape=(
            jax.ShapeDtypeStruct((width, np_rows), BF),
            jax.ShapeDtypeStruct((cut, width), F32),
        ),
        in_specs=[vmem()] * 8,
        out_specs=(vmem(), vmem()),
        scratch_shapes=[
            pltpu.VMEM((doms, width, blk), BF),
            pltpu.VMEM((mates, 2 * cut, width), BF),
            pltpu.VMEM((2, cut, width), F32),
            pltpu.VMEM((cut, width), F32),
            pltpu.VMEM((width, np_rows), F32),
            pltpu.VMEM((width, np_rows), BF),
            pltpu.VMEM((width, np_rows), BF),
            pltpu.VMEM((width, np_rows), BF),
            pltpu.VMEM((feats, width, np_rows), F32),
            pltpu.VMEM((PARTS, 2, last, width, np_rows // PARTS), BF),
            pltpu.VMEM((PARTS, 2, last, width, np_rows // PARTS), BF),
            pltpu.SemaphoreType.DMA((2,)),
            pltpu.SemaphoreType.DMA((2,)),
            pltpu.SemaphoreType.DMA((3, mates)),
            pltpu.SemaphoreType.DMA((3, mates)),
            pltpu.SemaphoreType.DMA((PARTS, 2, last)),
            pltpu.SemaphoreType.DMA((PARTS, 2, last)),
        ],
        compiler_params=linked(2),
    )(rows, rows_other, back, scaled_t, local_adj, grad_pre.T, w_pair, share)
    weight_scale = 1.0 / math.sqrt(doms * np_rows)
    return (output, grad_input_t.T, summed * weight_scale)


def solution(mesh):
    in_specs = (
        P("dom", "feat"),
        P(None, "feat"),
        P("dom", None, None),
        P("dom", None),
        P("dom", None),
        P("dom", None, None),
        P("dom"),
        P("dom", "feat"),
    )
    out_specs = (P("dom", "feat"), P("dom", "feat"), P("dom", "feat"))
    return jax.shard_map(
        per_device, mesh=mesh, in_specs=in_specs, out_specs=out_specs, check_vma=False
    )
```
